512 devices in a mesh: blk: 16 (over y_lo, x, core), seq: 32 (over z, y_hi).
Axes of the slice: x: 4, y: 8 (y_hi: 4, y_lo: 2; y = y_hi * 2 + y_lo), z: 8, core: 2. Of those that a mesh axis runs over, the one named last changes fastest.
Arguments:
- tokens: bfloat16 [65536, 8192], P(('blk', 'seq')), may hold values from -6 to 6
- seg_local: int32 [65536], P(('blk', 'seq')), may hold values from 0 to 15, as said below
- shard_counts: int32 [16, 32], P('blk', 'seq'), may hold values from 1 to 15, as said below
- norm_gain: float32 [8192], replicated, may hold values from 0.1 to 1.9
- query_weight: bfloat16 [8192, 8192], P('blk', 'seq'), may hold values from -1 to 1
- keyval_weight: bfloat16 [8192, 2, 1024], P('blk', None, 'seq'), may hold values from -4 to 4
Outputs:
- attended: bfloat16 [4096, 8192], P('blk', 'seq')
The draws below stay inside these ranges and needn't reach their ends.
Inputs may be any that keep to these rules, and one draw needn't show every extreme that they name: Within a shard seg_local never falls and rises by at most one from token to token; it counts the segment ends before the token on that shard, so a shard's tokens after its last end continue into the next shard's segment numbered 0 there. The last token of every group ends a segment. Every shard of a group has at least one end. `shard_counts`: the number of segment ends on the shard, equal to the number of distinct seg_local values of its tokens that end there; the counts of a group sum to 256, and in every group some shard has exactly 15.
All inputs are finite; a program needn't handle non-finite values.
Results may differ from the reference program's by a relative error of at most 0.0102.
The reference program's roundings to bfloat16 on the way (of `pooled`, `normed`, `queries`, `key_value`, `rotated_keys` and `weights`) count: a program that leaves them out, or rounds other values in their place, can miss the bound.
Values may be sent and summed in bfloat16 or wider, within the bound.
A program may use at most 64 MiB of HBM per device.

```python
import jax
import jax.numpy as jnp
from jax import lax

D = 8192
HEADS = 64
KV_HEADS = 8
HEAD = 128
TOK_DEV = 128
SEG_DEV = 8
TOKENS = 65536
N_BLK = 16
N_SEQ = 32


def segment_layout(key):
    base_key = jax.random.fold_in(key, 71)
    subkeys = jax.random.split(base_key, 3)
    half_seq = N_SEQ // 2
    spread = jax.random.randint(subkeys[0], (N_BLK, half_seq), -(SEG_DEV - 1), SEG_DEV)
    spread = spread.at[:, 0].set(SEG_DEV - 1)
    paired = jnp.concatenate([SEG_DEV + spread, SEG_DEV - spread], axis=1)
    order_scores = jax.random.randint(subkeys[1], (N_BLK, N_SEQ), 0, 1 << 20) * N_SEQ + jnp.arange(N_SEQ, dtype=jnp.int32)[None, :]
    shuffle = jnp.argsort(order_scores, axis=1)
    counts = jnp.take_along_axis(paired, shuffle, axis=1).astype(jnp.int32)
    place_scores = jax.random.randint(subkeys[2], (N_BLK, N_SEQ, TOK_DEV), 0, 1 << 16) * TOK_DEV + jnp.arange(TOK_DEV, dtype=jnp.int32)[None, None, :]
    last_seq = (jnp.arange(N_SEQ) == N_SEQ - 1)[None, :, None]
    last_tok = (jnp.arange(TOK_DEV) == TOK_DEV - 1)[None, None, :]
    place_scores = jnp.where(last_seq & last_tok, 1 << 28, place_scores)
    rank_of = jnp.argsort(jnp.argsort(-place_scores, axis=2), axis=2)
    seg_ends = (rank_of < counts[:, :, None]).astype(jnp.int32)
    local_ids = jnp.cumsum(seg_ends, axis=2) - seg_ends
    return (local_ids.reshape(N_BLK * N_SEQ * TOK_DEV).astype(jnp.int32), counts)


def draw_seg_local(key, part):
    return segment_layout(key)[0]


def draw_shard_counts(key, part):
    return segment_layout(key)[1]


def query_matrix(key):
    return jax.random.normal(jax.random.fold_in(key, 29), (D, HEADS * HEAD), jnp.float32) * D ** (-0.5)


def draw_query_weight(key, part):
    return jnp.clip(query_matrix(key), -1.0, 1.0).astype(jnp.bfloat16)


def draw_keyval_weight(key, part):
    jitter = jax.random.normal(jax.random.fold_in(key, 37), (D, 2, KV_HEADS * HEAD), jnp.float32) * D ** (-0.5)
    return jnp.clip(jitter, -4.0, 4.0).astype(jnp.bfloat16)


def block_scale(rng, dims, cuts, least, top_value):
    def one(position, blocks):
        draws = jax.random.uniform(jax.random.fold_in(jax.random.fold_in(rng, 6), position), (blocks,), jnp.float32, least / len(cuts), top_value / len(cuts))
        return jnp.repeat(jnp.exp(draws), dims[position] // blocks).reshape((-1,) + (1,) * (len(dims) - position - 1))

    level = one(*cuts[0])
    for cut in cuts[1:]:
        level = level * one(*cut)
    return level


def scatter_about(key, dims, width, most, pieces=(), kind=jnp.bfloat16):
    gain = block_scale(key, dims, pieces, -0.22, 0.18) if pieces else 1.0
    array = jax.random.normal(key, dims, jnp.float32) * width * gain
    return jnp.minimum(jnp.maximum(array, -most), most).astype(kind)


def setup_inputs(seed: int = 0) -> dict:
    key_list = jax.random.split(jax.random.key(seed), 7)
    return {
        "tokens": scatter_about(key_list[0], (TOKENS, D), 1.0, 6.0, ((0, 512),)),
        "seg_local": draw_seg_local(jax.random.fold_in(key_list[6], 71), 0),
        "shard_counts": draw_shard_counts(jax.random.fold_in(key_list[6], 71), 0),
        "norm_gain": jnp.clip(1.0 + 0.18 * jax.random.normal(key_list[3], (D,), jnp.float32), 0.1, 1.9),
        "query_weight": draw_query_weight(jax.random.fold_in(key_list[6], 71), 0),
        "keyval_weight": draw_keyval_weight(jax.random.fold_in(key_list[6], 71), 0),
    }


theta_base = 500000.0
norm_eps = 1e-05

def rotate(values_in, row_pos):
    half_dim = values_in.shape[-1] // 2
    frequency = theta_base ** (-(jnp.arange(half_dim, dtype=jnp.float32) * 2.0 / values_in.shape[-1]))
    angles = row_pos.astype(jnp.float32)[:, None] * frequency[None, :]
    cosine_table = jnp.cos(angles)[:, None, :]
    sine_table = jnp.sin(angles)[:, None, :]
    front_half = values_in[..., :half_dim]
    back_half = values_in[..., half_dim:]
    return jnp.concatenate([front_half * cosine_table - back_half * sine_table, back_half * cosine_table + front_half * sine_table], axis=-1)

def reference(tokens, seg_local, shard_counts, norm_gain, query_weight, keyval_weight):
    per_group = N_SEQ * SEG_DEV
    coarse = per_group * N_BLK
    prefix = (jnp.cumsum(shard_counts, axis=1) - shard_counts).astype(jnp.int32)
    segment_ids = seg_local.reshape(N_BLK, N_SEQ, TOK_DEV).astype(jnp.int32) + prefix[:, :, None]
    segment_ids = segment_ids.reshape(N_BLK, N_SEQ * TOK_DEV).astype(jnp.int32)
    grouped = tokens.reshape(N_BLK, N_SEQ * TOK_DEV, D)

    def pool_group(operand):
        group_tokens, group_ids = operand
        seg_sums = jax.ops.segment_sum(group_tokens.astype(jnp.float32), group_ids, num_segments=per_group)
        seg_sizes = jax.ops.segment_sum(jnp.ones(group_ids.shape, jnp.float32), group_ids, num_segments=per_group)
        return (seg_sums / seg_sizes[:, None]).astype(jnp.bfloat16)
    pooled = lax.map(pool_group, (grouped, segment_ids)).reshape(coarse, D)
    widened = pooled.astype(jnp.float32)
    normed = (widened * lax.rsqrt(lax.optimization_barrier(jnp.mean(widened * widened, axis=-1, keepdims=True)) + norm_eps) * norm_gain).astype(jnp.bfloat16)
    positions = jnp.arange(coarse, dtype=jnp.int32)
    queries = jnp.dot(normed, query_weight, preferred_element_type=jnp.float32).reshape(coarse, HEADS, HEAD)
    queries = rotate(queries, positions).astype(jnp.bfloat16)
    key_value = jnp.dot(normed, keyval_weight.reshape(D, 2 * KV_HEADS * HEAD), preferred_element_type=jnp.float32)
    key_value = key_value.reshape(coarse, 2, KV_HEADS, HEAD).astype(jnp.bfloat16)
    rotated_keys = rotate(key_value[:, 0].astype(jnp.float32), positions).astype(jnp.bfloat16)
    values = key_value[:, 1]
    group_size = HEADS // KV_HEADS
    score_scale = float(HEAD) ** (-0.5)
    causal = positions[None, :] <= positions[:, None]

    def one_head(head_index):
        query_head = lax.dynamic_index_in_dim(queries, head_index, 1, keepdims=False)
        key_head = lax.dynamic_index_in_dim(rotated_keys, head_index // group_size, 1, keepdims=False)
        value_head = lax.dynamic_index_in_dim(values, head_index // group_size, 1, keepdims=False)
        scores = jnp.dot(query_head, key_head.T, preferred_element_type=jnp.float32) * score_scale
        row_max = lax.optimization_barrier(jnp.max(jnp.where(causal, scores, -1e+30), axis=-1, keepdims=True))
        weights = jnp.where(causal, jnp.exp(scores - row_max), 0.0)
        row_sum = lax.optimization_barrier(jnp.sum(weights, axis=-1, keepdims=True))
        mixture = jnp.dot(weights.astype(jnp.bfloat16), value_head, preferred_element_type=jnp.float32)
        return (mixture / row_sum).astype(jnp.bfloat16)
    heads_out = lax.map(one_head, jnp.arange(HEADS, dtype=jnp.int32))
    return jnp.transpose(heads_out, (1, 0, 2)).reshape(coarse, HEADS * HEAD)
```

```python
import jax
import jax.numpy as jnp
from jax import lax
from jax.experimental import pallas as pl
from jax.experimental.pallas import tpu as pltpu
from jax.sharding import PartitionSpec as P

HEAD = 128
SLOTS = 16
COLS = 256
NZ, NY = 8, 4
NX, NYL, NC = 4, 2, 2
N_SEQ = NZ * NY
N_BLK = NYL * NX * NC
THETA = 500000.0
EPS = 1e-05
F32 = jnp.float32
BF16 = jnp.bfloat16


def rdma(src, dst, send, recv, where):
    return pltpu.make_async_remote_copy(
        src_ref=src, dst_ref=dst, send_sem=send, recv_sem=recv,
        device_id=where, device_id_type=pl.DeviceIdType.MESH,
    )


def blk_parts():
    blk = lax.axis_index("blk")
    return blk, blk // (NX * NC), (blk // NC) % NX, blk % NC


def blk_of(yl, x, c):
    return (yl * NX + x % NX) * NC + c


class PlaneGather:
    def __init__(self, buf, send, recv):
        self.buf, self.send, self.recv = buf, send, recv
        self.blk, self.yl, self.x, self.c = blk_parts()
        self.started = []

    def peers(self):
        return [
            blk_of(self.yl, self.x + 1, self.c), blk_of(self.yl, self.x + 3, self.c),
            blk_of(1 - self.yl, self.x, self.c), blk_of(self.yl, self.x, 1 - self.c),
        ]

    def move(self, sem, kind, dx, target):
        yl = self.yl if kind == 0 else 1 - self.yl
        origin = blk_of(yl, self.x + dx, self.c)
        copy = rdma(self.buf.at[origin], self.buf.at[origin], self.send.at[sem],
                    self.recv.at[sem], {"blk": target})
        copy.start()
        self.started.append(copy)

    def east(self, sem, kind, dx):
        self.move(sem, kind, dx, blk_of(self.yl, self.x + 1, self.c))

    def west(self, sem, kind, dx):
        self.move(sem, kind, dx, blk_of(self.yl, self.x + 3, self.c))

    def core(self, sem, kind, dx):
        self.move(sem, kind, dx, blk_of(self.yl, self.x, 1 - self.c))

    def arrive(self, sem):
        rdma(self.buf.at[0], self.buf.at[0], self.send.at[sem], self.recv.at[sem],
             {"blk": self.blk}).wait_recv()

    def phase0(self):
        self.east(1, 0, 0)
        self.west(2, 0, 0)
        self.core(7, 0, 0)

    def pair(self):
        self.move(0, 0, 0, blk_of(1 - self.yl, self.x, self.c))

    def phase1(self):
        self.arrive(1)
        self.east(3, 0, -1)
        self.core(8, 0, -1)
        self.arrive(2)
        self.core(9, 0, 1)

    def phase2(self):
        self.arrive(0)
        self.east(4, 1, 0)
        self.west(5, 1, 0)
        self.core(10, 1, 0)
        self.arrive(3)
        self.core(11, 0, 2)

    def phase3(self):
        self.arrive(5)
        self.west(6, 1, 1)
        self.core(12, 1, 1)
        self.arrive(4)
        self.core(13, 1, -1)

    def phase4(self):
        self.arrive(6)
        self.core(14, 1, 2)

    def finish(self):
        for sem in range(7, 15):
            self.arrive(sem)
        for copy in self.started:
            copy.wait_send()


def mm(a, b, dims=((1,), (0,))):
    return lax.dot_general(a, b, (dims, ((), ())), preferred_element_type=F32)


def iota(shape, axis):
    return lax.broadcasted_iota(jnp.int32, shape, axis)


def project_kernel(
    tokens, seg, count, weight, gain, cosine, sine, q_out, kv_out,
    main, extra, got_main, got_extra, rows, wbuf, squares, acc_q, acc_kv,
    a2a_send, a2a_recv, y_send, y_recv, z_send, z_recv, w_send, w_recv, local_sem,
):
    me = lax.axis_index("seq")
    z, y = me // NY, me % NY
    gather = PlaneGather(wbuf, w_send, w_recv)
    turn = 1 - 2 * gather.c

    def seq_of(zz, yy):
        return ((zz + 2 * NZ) % NZ) * NY + (yy + 2 * NY) % NY

    barrier = pltpu.get_barrier_semaphore()

    def greet(k, carry):
        pl.semaphore_signal(barrier, inc=1, device_id={"seq": (me + k) % N_SEQ},
                            device_id_type=pl.DeviceIdType.MESH)
        return carry

    lax.fori_loop(1, N_SEQ, greet, 0)
    for peer in gather.peers():
        pl.semaphore_signal(barrier, inc=1, device_id={"blk": peer},
                            device_id_type=pl.DeviceIdType.MESH)

    own_weight = pltpu.make_async_copy(weight, wbuf.at[gather.blk], local_sem)
    own_weight.start()

    slot = iota((SLOTS, 128), 0)
    member = (seg[...] == slot).astype(F32)
    sizes = jnp.sum(member, axis=1, keepdims=True)
    member = member.astype(BF16)
    is_tail = (slot == count[...]).astype(F32)
    tail_pick = is_tail[:, 0:1]
    tail_size = jnp.sum(sizes * is_tail, axis=0, keepdims=True)
    safe = jnp.maximum(sizes, 1.0)
    count_row = count[...].astype(F32)
    lead_size = jnp.broadcast_to(sizes[0:1], (1, 128))

    def pool(d, carry):
        column = pl.multiple_of(d * COLS, COLS)
        sums = mm(member, tokens[:, pl.ds(column, COLS)])
        main[d] = (sums / safe).astype(BF16)
        tail = jnp.sum(sums * tail_pick, axis=0, keepdims=True)
        extra[d] = jnp.concatenate(
            [sums[0:1, :128], sums[0:1, 128:], tail[:, :128], tail[:, 128:],
             count_row, lead_size, tail_size, jnp.zeros((1, 128), F32)], axis=0)
        return carry

    lax.fori_loop(0, N_SEQ, pool, 0)
    got_extra[0] = jnp.zeros((8, 128), F32)
    pl.semaphore_wait(barrier, N_SEQ - 1 + 4)

    def exchange(k):
        to = (me + k) % N_SEQ
        return (
            rdma(main.at[to], got_main.at[me], a2a_send.at[0, k], a2a_recv.at[0, k], {"seq": to}),
            rdma(extra.at[to], got_extra.at[me + 1], a2a_send.at[1, k], a2a_recv.at[1, k],
                 {"seq": to}),
        )

    def send_one(k, carry):
        for copy in exchange(k):
            copy.start()
        return carry

    def land_one(k, carry):
        for copy in exchange(k):
            copy.wait_recv()
        return carry

    def drain_one(k, carry):
        for copy in exchange(k):
            copy.wait_send()
        return carry

    lax.fori_loop(1, N_SEQ, send_one, 0)
    own_weight.wait()
    gather.phase0()
    got_main[me] = main[me]
    got_extra[me + 1] = extra[me]
    lax.fori_loop(1, N_SEQ, land_one, 0)

    total = N_SEQ * SLOTS
    counts = got_extra[1:N_SEQ + 1, 4, :]
    source = iota((N_SEQ, total), 0)
    owner = iota((N_SEQ, total), 1) // SLOTS
    counts16 = counts.astype(BF16)
    before = mm(counts16, (source < owner).astype(BF16), ((0,), (0,)))
    inside = mm(counts16, (source == owner).astype(BF16), ((0,), (0,)))
    rank = (iota((128, total), 1) % SLOTS).astype(F32)
    lead_sizes = got_extra[1:N_SEQ + 1, 5, :] + got_extra[0:N_SEQ, 6, :]
    border = jnp.concatenate(
        [(got_extra[1:N_SEQ + 1, i, :] + got_extra[0:N_SEQ, 2 + i, :]) / lead_sizes
         for i in range(2)], axis=1).astype(BF16)
    spread = (iota((total, N_SEQ), 0) // SLOTS == iota((total, N_SEQ), 1)).astype(BF16)
    slots = got_main[...].reshape(total, COLS)
    first = iota((total, COLS), 0) % SLOTS == 0
    slots = jnp.where(first, mm(spread, border), slots.astype(F32)).astype(BF16)
    for half in range(2):
        row = (iota((128, total), 0) + 128 * half).astype(F32)
        place = jnp.where(rank < inside, (before + rank == row).astype(F32), 0.0).astype(BF16)
        rows[me, pl.ds(128 * half, 128), :] = mm(place, slots).astype(BF16)

    lax.fori_loop(1, N_SEQ, drain_one, 0)

    started = []

    def y_step(sem, origin, step):
        copy = rdma(rows.at[origin], rows.at[origin], y_send.at[sem], y_recv.at[sem],
                    {"seq": seq_of(z, y + step)})
        copy.start()
        started.append(copy)

    def y_arrive(sem):
        rdma(rows.at[0], rows.at[0], y_send.at[sem], y_recv.at[sem], {"seq": me}).wait_recv()

    origin_y = (y, y - turn, y + turn, y + 2)
    hops = ((4, 3), (3, 4), (4, 3), (3, 4))

    def z_step(j, h):
        for side, step in ((0, 1), (1, -1)):
            if h < hops[j][side]:
                sem = (side * 4 + j) * 4 + h
                if h > 0:
                    z_arrive(j, h - 1, side)
                origin = seq_of(z - step * h, origin_y[j])
                copy = rdma(rows.at[origin], rows.at[origin], z_send.at[sem], z_recv.at[sem],
                            {"seq": seq_of(z + step, y)})
                copy.start()
                started.append(copy)

    def z_arrive(j, h, side):
        sem = (side * 4 + j) * 4 + h
        rdma(rows.at[0], rows.at[0], z_send.at[sem], z_recv.at[sem], {"seq": me}).wait_recv()

    z_step(0, 0)
    y_step(0, me, turn)
    y_step(1, me, -turn)
    gather.phase1()
    y_arrive(0)
    y_step(2, seq_of(z, y - turn), turn)
    z_step(1, 0)
    gather.pair()
    y_arrive(1)
    z_step(2, 0)
    z_step(0, 1)
    y_arrive(2)
    z_step(3, 0)
    z_step(1, 1)
    z_step(2, 1)
    gather.phase2()
    z_step(0, 2)
    z_step(3, 1)
    z_step(1, 2)
    gather.phase3()
    z_step(2, 2)
    z_step(3, 2)
    z_step(0, 3)
    gather.phase4()
    z_step(1, 3)
    z_step(2, 3)
    z_step(3, 3)
    gather.finish()
    for j in range(4):
        for side in range(2):
            z_arrive(j, hops[j][side] - 1, side)

    squares[...] = jnp.zeros_like(squares)

    def square(d, carry):
        piece = rows[d].astype(F32)
        squares[...] += piece * piece
        return carry

    lax.fori_loop(0, N_SEQ, square, 0)
    mean = jnp.sum(squares[...], axis=1, keepdims=True) * (1.0 / (N_SEQ * COLS))
    scale = lax.rsqrt(mean + EPS)
    acc_q[...] = jnp.zeros_like(acc_q)
    acc_kv[...] = jnp.zeros_like(acc_kv)

    def multiply(p, carry):
        for half in range(2):
            d = 2 * p + half
            normed = (rows[d].astype(F32) * scale * gain[pl.ds(d, 1), :]).astype(BF16)
            acc_q[...] += mm(normed, wbuf[p, pl.ds(256 * half, 256), :])
            acc_kv[...] += mm(wbuf[p, pl.ds(512 + 64 * half, 64), :], normed, ((1,), (1,)))
        return carry

    lax.fori_loop(0, N_BLK, multiply, 0)
    for head in range(2):
        one = acc_q[:, pl.ds(HEAD * head, HEAD)]
        turned = one * cosine[...] + pltpu.roll(one, HEAD // 2, 1) * sine[...]
        q_out[:, pl.ds(HEAD * head, HEAD)] = turned.astype(BF16)
    kv_out[...] = acc_kv[...].astype(BF16)
    for copy in started:
        copy.wait_send()


def spread_kernel(kv, cosine, sine, out, parts, q_send, q_recv, p_send, p_recv):
    me = lax.axis_index("seq")
    z, y = me // NY, me % NY
    gather = PlaneGather(out, p_send, p_recv)
    barrier = pltpu.get_barrier_semaphore()
    for k in range(1, NY):
        pl.semaphore_signal(barrier, inc=1, device_id={"seq": z * NY + (y + k) % NY},
                            device_id_type=pl.DeviceIdType.MESH)
    for peer in gather.peers():
        pl.semaphore_signal(barrier, inc=1, device_id={"blk": peer},
                            device_id_type=pl.DeviceIdType.MESH)
    pl.semaphore_wait(barrier, NY - 1 + 4)
    copies = [
        rdma(kv, parts.at[y], q_send.at[k], q_recv.at[k], {"seq": z * NY + (y + k) % NY})
        for k in range(1, NY)
    ]
    for copy in copies:
        copy.start()
    parts[y] = kv[...]
    for copy in copies:
        copy.wait()
    keys = jnp.concatenate([parts[i, pl.ds(0, 32), :] for i in range(NY)], axis=0).astype(F32)
    low, high = keys[:64], keys[64:]
    cos, sin = cosine[...], sine[...]
    mine = gather.blk
    out[mine, pl.ds(0, 64), :] = (low * cos - high * sin).astype(BF16)
    out[mine, pl.ds(64, 64), :] = (high * cos + low * sin).astype(BF16)
    for i in range(NY):
        out[mine, pl.ds(128 + 32 * i, 32), :] = parts[i, pl.ds(32, 32), :]
    gather.pair()
    gather.phase0()
    gather.phase1()
    gather.phase2()
    gather.phase3()
    gather.phase4()
    gather.finish()


def attend_kernel(q, kv, out, scores, peak, total, acc):
    blk = lax.axis_index("blk")
    unit = float(HEAD) ** (-0.5)
    for head in range(2):
        query = q[:, pl.ds(HEAD * head, HEAD)]
        peak[...] = jnp.full_like(peak, -1e30)

        def score(g, carry):
            s = mm(query, kv[g, pl.ds(0, HEAD), :]) * unit
            ok = g * 256 + iota((256, 256), 1) <= blk * 256 + iota((256, 256), 0)
            s = jnp.where(ok, s, -1e30)
            scores[g] = s
            peak[...] = jnp.maximum(peak[...], s)
            return carry

        lax.fori_loop(0, blk + 1, score, 0)
        top = jnp.max(peak[...], axis=1, keepdims=True)
        total[...] = jnp.zeros_like(total)
        acc[...] = jnp.zeros_like(acc)

        def mix(g, carry):
            w = jnp.exp(scores[g] - top)
            total[...] += w
            acc[...] += mm(w.astype(BF16), kv[g, pl.ds(HEAD, HEAD), :], ((1,), (1,)))
            return carry

        lax.fori_loop(0, blk + 1, mix, 0)
        norm = jnp.sum(total[...], axis=1, keepdims=True)
        out[:, pl.ds(HEAD * head, HEAD)] = (acc[...] / norm).astype(BF16)


def on_device(tokens, seg_local, shard_counts, norm_gain, query_weight, keyval_weight):
    rows_in_group = N_SEQ * 8
    vmem = pl.BlockSpec(memory_space=pltpu.VMEM)
    dma = pltpu.SemaphoreType.DMA
    blk = lax.axis_index("blk")
    positions = (blk * rows_in_group + jnp.arange(rows_in_group, dtype=jnp.int32)).astype(F32)
    half = HEAD // 2
    frequency = THETA ** (-(jnp.arange(half, dtype=F32) * 2.0 / HEAD))
    angles = positions[:, None] * frequency[None, :]
    cos, sin = jnp.cos(angles), jnp.sin(angles)
    cos2 = jnp.concatenate([cos, cos], axis=1)
    sin2 = jnp.concatenate([-sin, sin], axis=1)
    kv_t = keyval_weight.reshape(512, 64).T
    weight = jnp.concatenate([query_weight, kv_t[:, :256], kv_t[:, 256:]], axis=0)
    gain = norm_gain.reshape(N_SEQ, COLS)
    count = jnp.broadcast_to(shard_counts, (1, 128))
    q, kv = pl.pallas_call(
        project_kernel,
        out_shape=(
            jax.ShapeDtypeStruct((256, 256), BF16),
            jax.ShapeDtypeStruct((64, 256), BF16),
        ),
        in_specs=[vmem] * 7,
        out_specs=(vmem, vmem),
        scratch_shapes=[
            pltpu.VMEM((N_SEQ, SLOTS, COLS), BF16),
            pltpu.VMEM((N_SEQ, 8, 128), F32),
            pltpu.VMEM((N_SEQ, SLOTS, COLS), BF16),
            pltpu.VMEM((N_SEQ + 1, 8, 128), F32),
            pltpu.VMEM((N_SEQ, 256, COLS), BF16),
            pltpu.VMEM((N_BLK, 640, 256), BF16),
            pltpu.VMEM((256, COLS), F32),
            pltpu.VMEM((256, 256), F32),
            pltpu.VMEM((64, 256), F32),
            dma((2, N_SEQ)), dma((2, N_SEQ)),
            dma((3,)), dma((3,)),
            dma((32,)), dma((32,)),
            dma((15,)), dma((15,)),
            dma,
        ],
        compiler_params=pltpu.CompilerParams(
            collective_id=0, has_side_effects=True, vmem_limit_bytes=40 << 20),
        name="project",
    )(tokens, seg_local.reshape(1, 128), count, weight, gain, cos2, sin2)
    pieces = pl.pallas_call(
        spread_kernel,
        out_shape=jax.ShapeDtypeStruct((N_BLK, 256, 256), BF16),
        in_specs=[vmem] * 3,
        out_specs=vmem,
        scratch_shapes=[
            pltpu.VMEM((NY, 64, 256), BF16),
            dma((NY,)), dma((NY,)),
            dma((15,)), dma((15,)),
        ],
        compiler_params=pltpu.CompilerParams(
            collective_id=1, has_side_effects=True, vmem_limit_bytes=16 << 20),
        name="spread",
    )(kv, cos.T, sin.T)
    return pl.pallas_call(
        attend_kernel,
        out_shape=jax.ShapeDtypeStruct((256, 256), BF16),
        in_specs=[vmem] * 2,
        out_specs=vmem,
        scratch_shapes=[
            pltpu.VMEM((N_BLK, 256, 256), F32),
            pltpu.VMEM((256, 256), F32),
            pltpu.VMEM((256, 256), F32),
            pltpu.VMEM((256, HEAD), F32),
        ],
        compiler_params=pltpu.CompilerParams(vmem_limit_bytes=24 << 20),
        name="attend",
    )(q, pieces)


def solution(mesh):
    return jax.shard_map(
        on_device,
        mesh=mesh,
        in_specs=(
            P(("blk", "seq"), None),
            P(("blk", "seq")),
            P("blk", "seq"),
            P(),
            P("blk", "seq"),
            P("blk", None, "seq"),
        ),
        out_specs=P("blk", "seq"),
        check_vma=False,
    )
```

```python
import heapq

import jax
import jax.numpy as jnp
from jax import lax
from jax.experimental import pallas as pl
from jax.experimental.pallas import tpu as pltpu
from jax.sharding import PartitionSpec as P

HEAD = 128
SLOTS = 16
COLS = 256
NZ, NY = 8, 4
NX, NYL, NC = 4, 2, 2
N_SEQ = NZ * NY
N_BLK = NYL * NX * NC
UPPER = 176
THETA = 500000.0
EPS = 1e-05
F32 = jnp.float32
BF16 = jnp.bfloat16
MESH = pl.DeviceIdType.MESH


class Stream:
    def __init__(self, name, link, cost, lag, parent, make, group, delay=0.0):
        self.name, self.link, self.cost, self.lag = name, link, cost, lag
        self.parent, self.make, self.group, self.delay = parent, make, group, delay
        self.begun = False

    def start(self, started):
        self.begun = True
        copy = self.make()
        copy.start()
        started.append(copy)

    def arrive(self):
        self.make().wait_recv()


def schedule(streams):
    by_name = {s.name: i for i, s in enumerate(streams)}
    children = {i: [] for i in range(len(streams))}
    heap, actions = [], []
    for i, s in enumerate(streams):
        if s.parent is None:
            heap.append((s.delay, i))
        else:
            children[by_name[s.parent]].append(i)
    heapq.heapify(heap)
    free = {}
    while heap:
        ready, i = heapq.heappop(heap)
        s = streams[i]
        if s.parent is None and s.delay > 0.0:
            actions.append((ready, 0, i))
        end = max(ready, free.get(s.link, 0.0)) + s.cost
        free[s.link] = end
        actions.append((end + s.lag, 1, i))
        for c in children[i]:
            heapq.heappush(heap, (end + s.lag, c))
    return sorted(actions), children


def run(streams, started, after):
    actions, children = schedule(streams)
    for k, (time, kind, i) in enumerate(actions):
        if kind == 0:
            if not streams[i].begun:
                streams[i].start(started)
            continue
        streams[i].arrive()
        for c in children[i]:
            streams[c].start(started)
        later = [t for t, kd, j in actions[k + 1:] if kd == 0 or children[j]]
        after(streams[i], time, later[0] if later else None)


def rdma(src, dst, send, recv, where):
    return pltpu.make_async_remote_copy(
        src_ref=src, dst_ref=dst, send_sem=send, recv_sem=recv,
        device_id=where, device_id_type=MESH,
    )


def blk_parts():
    blk = lax.axis_index("blk")
    return blk, blk // (NX * NC), (blk // NC) % NX, blk % NC


def blk_of(yl, x, c):
    return (yl * NX + (x + NX) % NX) * NC + c


def plane_peers():
    _, yl, x, c = blk_parts()
    return [blk_of(yl, x + 1, c), blk_of(yl, x - 1, c), blk_of(1 - yl, x, c), blk_of(yl, x, 1 - c)]


PLANE = (
    ("east0", "east", None, 0, 0, 0),
    ("west0", "west", None, 0, 0, 1),
    ("core0", "core", None, 0, 0, 3),
    ("pair", "pair", None, 0, 0, 2),
    ("east1", "east", "east0", 0, -1, 0),
    ("core1", "core", "east0", 0, -1, 3),
    ("core2", "core", "west0", 0, 1, 3),
    ("core3", "core", "east1", 0, 2, 3),
    ("east2", "east", "pair", 1, 0, 0),
    ("west2", "west", "pair", 1, 0, 1),
    ("core4", "core", "pair", 1, 0, 3),
    ("west3", "west", "west2", 1, 1, 1),
    ("core5", "core", "west2", 1, 1, 3),
    ("core6", "core", "east2", 1, -1, 3),
    ("core7", "core", "west3", 1, 2, 3),
)
LANDS = {
    "east0": (0, -1, 0), "west0": (0, 1, 0), "core0": (0, 0, 1), "pair": (1, 0, 0),
    "east1": (0, 2, 0), "core1": (0, -1, 1), "core2": (0, 1, 1), "core3": (0, 2, 1),
    "east2": (1, -1, 0), "west2": (1, 1, 0), "core4": (1, 0, 1), "west3": (1, 2, 0),
    "core5": (1, 1, 1), "core6": (1, -1, 1), "core7": (1, 2, 1),
}


def plane_streams(buf, send, recv, cost, parts, group, pair_delay):
    _, yl, x, c = blk_parts()
    targets = plane_peers()
    streams = []
    for p, (first, size) in enumerate(parts):
        for i, (name, link, parent, kind, dx, target) in enumerate(PLANE):
            origin = blk_of(yl if kind == 0 else 1 - yl, x + dx, c)
            piece = buf.at[origin, pl.ds(first, size)]
            sem = p * len(PLANE) + i

            def make(piece=piece, sem=sem, target=target):
                return rdma(piece, piece, send.at[sem], recv.at[sem], {"blk": targets[target]})

            streams.append(Stream(
                (name, p), link, cost / 5 if link == "core" else cost,
                1.0 if link == "core" else 1.7, None if parent is None else (parent, p), make,
                (group, name), pair_delay if name == "pair" else 0.0))
    return streams


def mm(a, b, dims=((1,), (0,))):
    return lax.dot_general(a, b, (dims, ((), ())), preferred_element_type=F32)


def iota(shape, axis):
    return lax.broadcasted_iota(jnp.int32, shape, axis)


def layer_kernel(
    tokens, seg, count, q_weight, kv_weight, gain, cosine, sine, cos_t, sin_t, out,
    tok, main, extra, got_main, got_extra, sq, got_sq, rows, wbuf, scale, acc_q, acc_kv,
    query, kv, parts, keys, top, total, acc,
    tok_sem, own_sem, a2a_send, a2a_recv, sq_send, sq_recv, r_send, r_recv,
    w_send, w_recv, quad_send, quad_recv, k_send, k_recv,
):
    me = lax.axis_index("seq")
    z, y = me // NY, me % NY
    blk, yl, x, core = blk_parts()
    turn = 1 - 2 * core

    def seq_of(zz, yy):
        return ((zz + 2 * NZ) % NZ) * NY + (yy + 2 * NY) % NY

    barrier = pltpu.get_barrier_semaphore()

    def greet(k, carry):
        pl.semaphore_signal(barrier, inc=1, device_id={"seq": (me + k) % N_SEQ},
                            device_id_type=MESH)
        return carry

    chunk = N_SEQ * COLS // 4
    token_loads = [
        pltpu.make_async_copy(tokens.at[:, pl.ds(i * chunk, chunk)],
                              tok.at[:, pl.ds(i * chunk, chunk)], tok_sem.at[i])
        for i in range(4)
    ]
    own_loads = [
        pltpu.make_async_copy(q_weight, wbuf.at[blk, pl.ds(0, 512)], own_sem.at[0]),
        pltpu.make_async_copy(kv_weight.at[:, pl.ds(0, 256)], wbuf.at[blk, pl.ds(512, 64)],
                              own_sem.at[1]),
        pltpu.make_async_copy(kv_weight.at[:, pl.ds(256, 256)], wbuf.at[blk, pl.ds(576, 64)],
                              own_sem.at[2]),
    ]
    for load in token_loads + own_loads:
        load.start()
    lax.fori_loop(1, N_SEQ, greet, 0)
    for peer in plane_peers():
        pl.semaphore_signal(barrier, inc=1, device_id={"blk": peer}, device_id_type=MESH)

    slot = iota((SLOTS, 128), 0)
    member = (seg[...] == slot).astype(F32)
    sizes = jnp.sum(member, axis=1, keepdims=True)
    member = member.astype(BF16)
    is_tail = (slot == count[...]).astype(F32)
    tail_pick = is_tail[:, 0:1]
    tail_size = jnp.sum(sizes * is_tail, axis=0, keepdims=True)
    safe = jnp.maximum(sizes, 1.0)
    count_row = count[...].astype(F32)
    lead_size = jnp.broadcast_to(sizes[0:1], (1, 128))

    def pool(d, carry):
        column = pl.multiple_of(d * COLS, COLS)
        sums = mm(member, tok[:, pl.ds(column, COLS)])
        main[d] = (sums / safe).astype(BF16)
        tail = jnp.sum(sums * tail_pick, axis=0, keepdims=True)
        extra[d] = jnp.concatenate(
            [sums[0:1, :128], sums[0:1, 128:], tail[:, :128], tail[:, 128:],
             count_row, lead_size, tail_size, jnp.zeros((1, 128), F32)], axis=0)
        return carry

    for i in range(4):
        token_loads[i].wait()
        lax.fori_loop(8 * i, 8 * i + 8, pool, 0)
    got_extra[0] = jnp.zeros((8, 128), F32)
    for load in own_loads:
        load.wait()
    pl.semaphore_wait(barrier, N_SEQ - 1 + 4)

    def exchange(k):
        to = (me + k) % N_SEQ
        return (
            rdma(main.at[to], got_main.at[me], a2a_send.at[0, k], a2a_recv.at[0, k], {"seq": to}),
            rdma(extra.at[to], got_extra.at[me + 1], a2a_send.at[1, k], a2a_recv.at[1, k],
                 {"seq": to}),
        )

    def share(k):
        return (rdma(sq, got_sq.at[me], sq_send.at[k], sq_recv.at[k], {"seq": (me + k) % N_SEQ}),)

    def each(copies, what):
        def body(k, carry):
            for copy in copies(k):
                getattr(copy, what)()
            return carry

        lax.fori_loop(1, N_SEQ, body, 0)

    started = []
    weights = plane_streams(wbuf, w_send, w_recv, 7.3, ((0, 640),), "weight", 12.0)
    each(exchange, "start")
    for s in weights:
        if s.parent is None and s.delay == 0.0:
            s.start(started)
    got_main[me] = main[me]
    got_extra[me + 1] = extra[me]
    each(exchange, "wait_recv")

    slots_all = N_SEQ * SLOTS
    counts16 = got_extra[1:N_SEQ + 1, 4, :].astype(BF16)
    source = iota((N_SEQ, slots_all), 0)
    owner = iota((N_SEQ, slots_all), 1) // SLOTS
    before = mm(counts16, (source < owner).astype(BF16), ((0,), (0,)))
    inside = mm(counts16, (source == owner).astype(BF16), ((0,), (0,)))
    rank = (iota((128, slots_all), 1) % SLOTS).astype(F32)
    lead_sizes = got_extra[1:N_SEQ + 1, 5, :] + got_extra[0:N_SEQ, 6, :]
    border = jnp.concatenate(
        [(got_extra[1:N_SEQ + 1, i, :] + got_extra[0:N_SEQ, 2 + i, :]) / lead_sizes
         for i in range(2)], axis=1).astype(BF16)
    spread = (iota((slots_all, N_SEQ), 0) // SLOTS == iota((slots_all, N_SEQ), 1)).astype(BF16)
    slots = got_main[...].reshape(slots_all, COLS)
    first = iota((slots_all, COLS), 0) % SLOTS == 0
    slots = jnp.where(first, mm(spread, border), slots.astype(F32)).astype(BF16)
    ones = jnp.ones((8, COLS), BF16)
    for half in range(2):
        row = (iota((128, slots_all), 0) + 128 * half).astype(F32)
        place = jnp.where(rank < inside, (before + rank == row).astype(F32), 0.0).astype(BF16)
        rows[me, pl.ds(128 * half, 128), :] = mm(place, slots).astype(BF16)
    for half in range(2):
        piece = rows[me, pl.ds(128 * half, 128), :].astype(F32)
        square = piece * piece
        coarse = square.astype(BF16)
        fine = (square - coarse.astype(F32)).astype(BF16)
        across = mm(ones, coarse, ((1,), (1,))) + mm(ones, fine, ((1,), (1,)))
        sq[half:half + 1, :] = across[0:1]

    streams = list(weights)
    counter = [0]

    def add(name, link, cost, lag, parent, part, origin, target, group):
        sem = counter[0]
        counter[0] += 1
        at, size = ((0, UPPER), (UPPER, 256 - UPPER))[part]
        piece = rows.at[seq_of(z + origin[0], y + origin[1]), pl.ds(at, size)]
        where = {"seq": seq_of(z + target[0], y + target[1])}

        def make():
            return rdma(piece, piece, r_send.at[sem], r_recv.at[sem], where)

        streams.append(Stream(name, link, cost, lag, parent, make, ("row", group),
                              13.0 if parent is None else 0.0))

    zc, yc = (2.0, 0.95), (2.0, 0.95)
    dys = (0, -turn, turn, 2)
    hops = ((4, 3), (3, 4), (4, 3), (3, 4))
    own = ("yA", "yB", "yC")

    def z_upper(j, h):
        for side, step in ((0, 1), (1, -1)):
            if h < hops[j][side]:
                parent = ("z", j, side, h - 1) if h else (None if j == 0 else own[j - 1])
                add(("z", j, side, h), "z%d" % side, zc[0], 1.7, parent, 0,
                    (-step * h, dys[j]), (step, 0), h + 1)

    def y_all(tag, parent, part, dz, group):
        names = own if tag is None else tuple((n, tag) for n in own)
        add(names[0], "y", yc[part], 2.4, parent, part, (dz, 0), (0, turn), group)
        add(names[1], "y", yc[part], 2.4, parent, part, (dz, 0), (0, -turn), group)
        add(names[2], "y", yc[part], 2.4, names[0], part, (dz, -turn), (0, turn), group)

    z_upper(0, 0)
    y_all(None, None, 0, 0, 0)
    for side, step in ((0, turn), (1, -turn)):
        for h in range((4, 3)[side]):
            add(("zz", side, h), "z%d" % side, zc[1], 1.7, ("zz", side, h - 1) if h else None, 1,
                (-step * h, 0), (step, 0), h + 1)
            y_all(("zz", side, h), ("zz", side, h), 1, -step * (h + 1), h + 1)
    y_all("zz", None, 1, 0, 0)
    for h in range(4):
        for j in range(4):
            if (j, h) != (0, 0):
                z_upper(j, h)

    for s in streams[len(weights):]:
        if s.parent is None:
            s.start(started)
    each(share, "start")
    got_sq[me] = sq[...]
    each(exchange, "wait_send")
    acc_q[...] = jnp.zeros_like(acc_q)
    acc_kv[...] = jnp.zeros_like(acc_kv)
    left = {}
    for s in streams:
        kind = s.group[0] if s.group[0] == "weight" else s.group[1]
        left[kind] = left.get(kind, 0) + 1
    scaled = []

    def scale_rows():
        each(share, "wait_recv")
        mean = jnp.sum(got_sq[...], axis=0) * (1.0 / (N_SEQ * COLS))
        inverse = lax.rsqrt(mean + EPS)
        eye = iota((128, 128), 0) == iota((128, 128), 1)
        for half in range(2):
            line = jnp.broadcast_to(inverse[half:half + 1], (128, 128))
            column = jnp.sum(jnp.where(eye, line, 0.0), axis=1, keepdims=True)
            scale[pl.ds(128 * half, 128), :] = jnp.broadcast_to(column, (128, 128))

    def multiply(h, n):
        def body(i, carry):
            sign = 1 - 2 * (i // NY)
            d = ((z + sign * h + NZ) % NZ) * NY + i % NY
            gains = gain[0:1, pl.ds(pl.multiple_of(d * COLS, COLS), COLS)]
            wide = jnp.concatenate([scale[...], scale[...]], axis=1)
            normed = (rows[d].astype(F32) * wide * gains).astype(BF16)
            p, half = d // 2, d % 2
            q_at = pl.multiple_of(half * 256, 256)
            kv_at = pl.multiple_of(512 + half * 64, 64)
            acc_q[...] += mm(normed, wbuf[p, pl.ds(q_at, 256), :])
            acc_kv[...] += mm(wbuf[p, pl.ds(kv_at, 64), :], normed, ((1,), (1,)))
            return carry

        lax.fori_loop(0, n, body, 0)

    waiting = [0, 1, 2, 3, 4]

    def row_step(stream, time, later):
        kind = stream.group[0] if stream.group[0] == "weight" else stream.group[1]
        left[kind] -= 1
        if left["weight"]:
            return
        for h in list(waiting):
            if left[h] == 0:
                if not scaled:
                    scaled.append(scale_rows())
                multiply(h, 4 if h in (0, 4) else 8)
                waiting.remove(h)

    run(streams, started, row_step)
    assert not waiting

    def turn_query(head):
        one = acc_q[:, pl.ds(HEAD * head, HEAD)]
        turned = one * cosine[...] + pltpu.roll(one, HEAD // 2, 1) * sine[...]
        query[head] = turned.astype(BF16)

    kv[...] = acc_kv[...].astype(BF16)
    turn_query(0)
    quad = [
        rdma(kv, parts.at[y], quad_send.at[k], quad_recv.at[k], {"seq": z * NY + (y + k) % NY})
        for k in range(1, NY)
    ]
    for copy in quad:
        copy.start()
    parts[y] = kv[...]
    turn_query(1)
    for copy in quad:
        copy.wait()
    both = jnp.concatenate([parts[i, pl.ds(0, 32), :] for i in range(NY)], axis=0).astype(F32)
    low, high = both[:64], both[64:]
    cos, sin = cos_t[...], sin_t[...]
    keys[blk, pl.ds(0, 64), :] = (low * cos - high * sin).astype(BF16)
    keys[blk, pl.ds(64, 64), :] = (high * cos + low * sin).astype(BF16)
    for i in range(NY):
        keys[blk, pl.ds(128 + 32 * i, 32), :] = parts[i, pl.ds(32, 32), :]

    key_streams = plane_streams(keys, k_send, k_recv, 1.5, ((0, 128), (128, 128)), "key", 0.0)
    for s in key_streams:
        if s.parent is None:
            s.start(started)

    unit = float(HEAD) ** (-0.5)

    def attend(origin, diagonal):
        for head in range(2):
            s = mm(query[head], keys[origin, pl.ds(0, HEAD), :]) * unit
            if diagonal:
                s = jnp.where(iota((256, 256), 1) <= iota((256, 256), 0), s, -1e30)
            high = jnp.max(s, axis=1, keepdims=True)
            if diagonal:
                new = jnp.broadcast_to(high, (256, HEAD))
            else:
                old = top[head]
                new = jnp.maximum(old, high)
                fade = jnp.exp(old - new)
            w = jnp.exp(s - jnp.concatenate([new, new], axis=1))
            part = w[:, :HEAD] + w[:, HEAD:]
            mix = mm(w.astype(BF16), keys[origin, pl.ds(HEAD, HEAD), :], ((1,), (1,)))
            top[head] = new
            total[head] = part if diagonal else total[head] * fade + part
            acc[head] = mix if diagonal else acc[head] * fade + mix

    attend(blk, True)
    seen, ready = {}, []
    clock = [1.0]

    def attend_earlier(name):
        kind, dx, other = LANDS[name]
        origin = blk_of(yl if kind == 0 else 1 - yl, x + dx, 1 - core if other else core)

        @pl.when(origin < blk)
        def _():
            attend(origin, False)

    def key_step(stream, time, later):
        name = stream.group[1]
        seen[name] = seen.get(name, 0) + 1
        if seen[name] == 2:
            ready.append(name)
        clock[0] = max(clock[0], time)
        while ready and (later is None or clock[0] + 0.6 <= later):
            attend_earlier(ready.pop(0))
            clock[0] += 0.6

    run(key_streams, started, key_step)
    for name in ready:
        attend_earlier(name)
    for head in range(2):
        norm = jnp.sum(total[head], axis=1, keepdims=True)
        out[:, pl.ds(HEAD * head, HEAD)] = (acc[head] / norm).astype(BF16)
    for copy in started:
        copy.wait_send()
    each(share, "wait_send")


def on_device(tokens, seg_local, shard_counts, norm_gain, query_weight, keyval_weight):
    rows_in_group = N_SEQ * 8
    vmem = pl.BlockSpec(memory_space=pltpu.VMEM)
    anywhere = pl.BlockSpec(memory_space=pltpu.HBM)
    dma = pltpu.SemaphoreType.DMA
    blk = lax.axis_index("blk")
    positions = (blk * rows_in_group + jnp.arange(rows_in_group, dtype=jnp.int32)).astype(F32)
    half = HEAD // 2
    frequency = THETA ** (-(jnp.arange(half, dtype=F32) * 2.0 / HEAD))
    angles = positions[:, None] * frequency[None, :]
    cos, sin = jnp.cos(angles), jnp.sin(angles)
    cos2 = jnp.concatenate([cos, cos], axis=1)
    sin2 = jnp.concatenate([-sin, sin], axis=1)
    kv_t = keyval_weight.reshape(512, 64).T
    return pl.pallas_call(
        layer_kernel,
        out_shape=jax.ShapeDtypeStruct((256, 256), BF16),
        in_specs=[anywhere, vmem, vmem, anywhere, anywhere] + [vmem] * 5,
        out_specs=vmem,
        scratch_shapes=[
            pltpu.VMEM((128, N_SEQ * COLS), BF16),
            pltpu.VMEM((N_SEQ, SLOTS, COLS), BF16),
            pltpu.VMEM((N_SEQ, 8, 128), F32),
            pltpu.VMEM((N_SEQ, SLOTS, COLS), BF16),
            pltpu.VMEM((N_SEQ + 1, 8, 128), F32),
            pltpu.VMEM((2, 128), F32),
            pltpu.VMEM((N_SEQ, 2, 128), F32),
            pltpu.VMEM((N_SEQ, 256, COLS), BF16),
            pltpu.VMEM((N_BLK, 640, 256), BF16),
            pltpu.VMEM((256, 128), F32),
            pltpu.VMEM((256, 256), F32),
            pltpu.VMEM((64, 256), F32),
            pltpu.VMEM((2, 256, HEAD), BF16),
            pltpu.VMEM((64, 256), BF16),
            pltpu.VMEM((NY, 64, 256), BF16),
            pltpu.VMEM((N_BLK, 256, 256), BF16),
            pltpu.VMEM((2, 256, HEAD), F32),
            pltpu.VMEM((2, 256, HEAD), F32),
            pltpu.VMEM((2, 256, HEAD), F32),
            dma((4,)), dma((3,)),
            dma((2, N_SEQ)), dma((2, N_SEQ)),
            dma((N_SEQ,)), dma((N_SEQ,)),
            dma((62,)), dma((62,)),
            dma((15,)), dma((15,)),
            dma((NY,)), dma((NY,)),
            dma((30,)), dma((30,)),
        ],
        compiler_params=pltpu.CompilerParams(
            collective_id=0, has_side_effects=True, vmem_limit_bytes=48 << 20),
        name="layer",
    )(tokens, seg_local.reshape(1, 128), jnp.broadcast_to(shard_counts, (1, 128)), query_weight,
      kv_t, norm_gain.reshape(1, N_SEQ * COLS), cos2, sin2, cos.T, sin.T)


def solution(mesh):
    return jax.shard_map(
        on_device,
        mesh=mesh,
        in_specs=(
            P(("blk", "seq"), None),
            P(("blk", "seq")),
            P("blk", "seq"),
            P(),
            P("blk", "seq"),
            P("blk", None, "seq"),
        ),
        out_specs=P("blk", "seq"),
        check_vma=False,
    )
```

```python
import heapq

import jax
import jax.numpy as jnp
from jax import lax
from jax.experimental import pallas as pl
from jax.experimental.pallas import tpu as pltpu
from jax.sharding import PartitionSpec as P

HEAD = 128
SLOTS = 16
COLS = 256
NZ, NY = 8, 4
NX, NYL, NC = 4, 2, 2
N_SEQ = NZ * NY
N_BLK = NYL * NX * NC
UPPER = 192
THETA = 500000.0
EPS = 1e-05
F32 = jnp.float32
BF16 = jnp.bfloat16
MESH = pl.DeviceIdType.MESH


class Stream:
    def __init__(self, name, link, cost, lag, parent, make, group, delay=0.0):
        self.name, self.link, self.cost, self.lag = name, link, cost, lag
        self.parent, self.make, self.group, self.delay = parent, make, group, delay
        self.begun = False

    def start(self, started):
        self.begun = True
        copy = self.make()
        copy.start()
        started.append(copy)

    def arrive(self):
        self.make().wait_recv()


def schedule(streams, margin):
    by_name = {s.name: i for i, s in enumerate(streams)}
    children = {i: [] for i in range(len(streams))}
    heap, actions = [], []
    for i, s in enumerate(streams):
        if s.parent is None:
            heap.append((s.delay, i))
        else:
            children[by_name[s.parent]].append(i)
    heapq.heapify(heap)
    free = {}
    while heap:
        ready, i = heapq.heappop(heap)
        s = streams[i]
        if s.parent is None and s.delay > 0.0:
            actions.append((ready, 0, i))
        end = max(ready, free.get(s.link, 0.0)) + s.cost
        free[s.link] = end
        actions.append((end + s.lag + (0.0 if children[i] else margin), 1, i))
        for c in children[i]:
            heapq.heappush(heap, (end + s.lag, c))
    return sorted(actions), children


def drive(streams, plan, first, limit, started, after):
    actions, children = plan
    for k in range(first, len(actions)):
        time, kind, i = actions[k]
        if limit is not None and time > limit:
            return k
        if kind == 0:
            if not streams[i].begun:
                streams[i].start(started)
            continue
        streams[i].arrive()
        for c in children[i]:
            streams[c].start(started)
        later = [t for t, kd, j in actions[k + 1:] if kd == 0 or children[j]]
        after(streams[i], time, later[0] if later else None)
    return len(actions)


def rdma(src, dst, send, recv, where):
    return pltpu.make_async_remote_copy(
        src_ref=src, dst_ref=dst, send_sem=send, recv_sem=recv,
        device_id=where, device_id_type=MESH,
    )


def blk_parts():
    blk = lax.axis_index("blk")
    return blk, blk // (NX * NC), (blk // NC) % NX, blk % NC


def blk_of(yl, x, c):
    return (yl * NX + (x + NX) % NX) * NC + c


def plane_peers():
    _, yl, x, c = blk_parts()
    return [blk_of(yl, x + 1, c), blk_of(yl, x - 1, c), blk_of(1 - yl, x, c), blk_of(yl, x, 1 - c)]


PLANE = (
    ("east0", "east", None, 0, 0, 0),
    ("west0", "west", None, 0, 0, 1),
    ("core0", "core", None, 0, 0, 3),
    ("pair", "pair", None, 0, 0, 2),
    ("east1", "east", "east0", 0, -1, 0),
    ("core1", "core", "east0", 0, -1, 3),
    ("core2", "core", "west0", 0, 1, 3),
    ("core3", "core", "east1", 0, 2, 3),
    ("east2", "east", "pair", 1, 0, 0),
    ("west2", "west", "pair", 1, 0, 1),
    ("core4", "core", "pair", 1, 0, 3),
    ("west3", "west", "west2", 1, 1, 1),
    ("core5", "core", "west2", 1, 1, 3),
    ("core6", "core", "east2", 1, -1, 3),
    ("core7", "core", "west3", 1, 2, 3),
)
LANDS = {
    "east0": (0, -1, 0), "west0": (0, 1, 0), "core0": (0, 0, 1), "pair": (1, 0, 0),
    "east1": (0, 2, 0), "core1": (0, -1, 1), "core2": (0, 1, 1), "core3": (0, 2, 1),
    "east2": (1, -1, 0), "west2": (1, 1, 0), "core4": (1, 0, 1), "west3": (1, 2, 0),
    "core5": (1, 1, 1), "core6": (1, -1, 1), "core7": (1, 2, 1),
}


def plane_streams(buf, send, recv, cost, parts, group, pair_delay):
    _, yl, x, c = blk_parts()
    targets = plane_peers()
    streams = []
    for p, (first, size) in enumerate(parts):
        for i, (name, link, parent, kind, dx, target) in enumerate(PLANE):
            origin = blk_of(yl if kind == 0 else 1 - yl, x + dx, c)
            piece = buf.at[origin, pl.ds(first, size)]
            sem = p * len(PLANE) + i

            def make(piece=piece, sem=sem, target=target):
                return rdma(piece, piece, send.at[sem], recv.at[sem], {"blk": targets[target]})

            streams.append(Stream(
                (name, p), link, cost / 5 if link == "core" else cost,
                1.0 if link == "core" else 1.7, None if parent is None else (parent, p), make,
                (group, name), pair_delay if name == "pair" else 0.0))
    return streams


def mm(a, b, dims=((1,), (0,))):
    return lax.dot_general(a, b, (dims, ((), ())), preferred_element_type=F32)


def iota(shape, axis):
    return lax.broadcasted_iota(jnp.int32, shape, axis)


def layer_kernel(
    tokens, seg_hbm, count_hbm, q_weight, kv_weight, gain_hbm, freq_hbm, out,
    seg, count, gain, freq, cosine, sine, cos_t, sin_t, tok, main, extra, got_main, got_extra, sq, got_sq, rows, wbuf, scale, acc_q, acc_kv,
    query, kv, parts, keys, top, total, acc,
    small_sem, tok_sem, own_sem, a2a_send, a2a_recv, sq_send, sq_recv, r_send, r_recv,
    w_send, w_recv, quad_send, quad_recv, k_send, k_recv,
):
    me = lax.axis_index("seq")
    z, y = me // NY, me % NY
    blk, yl, x, core = blk_parts()
    turn = 1 - 2 * core

    def seq_of(zz, yy):
        return ((zz + 2 * NZ) % NZ) * NY + (yy + 2 * NY) % NY

    barrier = pltpu.get_barrier_semaphore()

    def greet(k, carry):
        pl.semaphore_signal(barrier, inc=1, device_id={"seq": (me + k) % N_SEQ},
                            device_id_type=MESH)
        return carry

    chunk = N_SEQ * COLS // 4
    token_loads = [
        pltpu.make_async_copy(tokens.at[:, pl.ds(i * chunk, chunk)],
                              tok.at[:, pl.ds(i * chunk, chunk)], tok_sem.at[i])
        for i in range(4)
    ]
    own_loads = [
        pltpu.make_async_copy(q_weight, wbuf.at[blk, pl.ds(0, 512)], own_sem.at[0]),
        pltpu.make_async_copy(kv_weight.at[:, pl.ds(0, 256)], wbuf.at[blk, pl.ds(512, 64)],
                              own_sem.at[1]),
        pltpu.make_async_copy(kv_weight.at[:, pl.ds(256, 256)], wbuf.at[blk, pl.ds(576, 64)],
                              own_sem.at[2]),
    ]
    smalls = [
        pltpu.make_async_copy(src, dst, small_sem.at[i])
        for i, (src, dst) in enumerate((
            (seg_hbm, seg), (count_hbm, count), (gain_hbm, gain), (freq_hbm, freq)))
    ]
    for load in smalls[:2] + token_loads + own_loads + smalls[2:]:
        load.start()
    lax.fori_loop(1, N_SEQ, greet, 0)
    for peer in plane_peers():
        pl.semaphore_signal(barrier, inc=1, device_id={"blk": peer}, device_id_type=MESH)

    for load in smalls[:2]:
        load.wait()
    slot = iota((SLOTS, 128), 0)
    member = (seg[...] == slot).astype(F32)
    sizes = jnp.sum(member, axis=1, keepdims=True)
    member = member.astype(BF16)
    is_tail = (slot == count[...]).astype(F32)
    tail_pick = is_tail[:, 0:1]
    tail_size = jnp.sum(sizes * is_tail, axis=0, keepdims=True)
    safe = jnp.maximum(sizes, 1.0)
    meta = jnp.concatenate(
        [count[...].astype(F32), jnp.broadcast_to(sizes[0:1], (1, 64)), tail_size[:, :64]], axis=1)
    top_row = iota((SLOTS, COLS), 0) == 0

    for i in range(4):
        token_loads[i].wait()
        for d in range(8 * i, 8 * i + 8):
            sums = mm(member, tok[:, pl.ds(d * COLS, COLS)])
            main[d] = jnp.where(top_row, meta, sums / safe).astype(BF16)
            tail = jnp.sum(sums * tail_pick, axis=0, keepdims=True)
            extra[d] = jnp.concatenate(
                [sums[0:1, :128], sums[0:1, 128:], tail[:, :128], tail[:, 128:]], axis=0)
    got_extra[0] = jnp.zeros((4, 128), F32)
    for load in own_loads + smalls[2:]:
        load.wait()
    pl.semaphore_wait(barrier, N_SEQ - 1 + 4)

    def exchange(k):
        to = (me + k) % N_SEQ
        return (
            rdma(main.at[to], got_main.at[me], a2a_send.at[0, k], a2a_recv.at[0, k], {"seq": to}),
            rdma(extra.at[to], got_extra.at[me + 1], a2a_send.at[1, k], a2a_recv.at[1, k],
                 {"seq": to}),
        )

    def share(k):
        return (rdma(sq, got_sq.at[me], sq_send.at[k], sq_recv.at[k], {"seq": (me + k) % N_SEQ}),)

    def each(copies, what):
        def body(k, carry):
            for copy in copies(k):
                getattr(copy, what)()
            return carry

        lax.fori_loop(1, N_SEQ, body, 0)

    started = []
    weights = plane_streams(wbuf, w_send, w_recv, 1.9, [(160 * i, 160) for i in range(4)],
                            "weight", 0.0)
    streams = list(weights)
    counter = [0]

    def add(name, link, cost, lag, parent, part, origin, target, group):
        sem = counter[0]
        counter[0] += 1
        at, size = ((0, UPPER), (UPPER, 256 - UPPER))[part]
        piece = rows.at[seq_of(z + origin[0], y + origin[1]), pl.ds(at, size)]
        where = {"seq": seq_of(z + target[0], y + target[1])}

        def make():
            return rdma(piece, piece, r_send.at[sem], r_recv.at[sem], where)

        streams.append(Stream(name, link, cost, lag, parent, make, ("row", group),
                              13.0 if parent is None else 0.0))

    zc = (0.01138 * UPPER, 0.01138 * (256 - UPPER))
    yc = (0.0125 * UPPER, 0.0125 * (256 - UPPER))
    dys = (0, -turn, turn, 2)
    hops = ((4, 3), (3, 4), (4, 3), (3, 4))
    own = ("yA", "yB", "yC")

    def z_upper(j, h):
        for side, step in ((0, 1), (1, -1)):
            if h < hops[j][side]:
                parent = ("z", j, side, h - 1) if h else (None if j == 0 else own[j - 1])
                add(("z", j, side, h), "z%d" % side, zc[0], 1.7, parent, 0,
                    (-step * h, dys[j]), (step, 0), h + 1)

    def y_all(tag, parent, part, dz, group):
        names = own if tag is None else tuple((n, tag) for n in own)
        add(names[0], "y", yc[part], 2.4, parent, part, (dz, 0), (0, turn), group)
        add(names[1], "y", yc[part], 2.4, parent, part, (dz, 0), (0, -turn), group)
        add(names[2], "y", yc[part], 2.4, names[0], part, (dz, -turn), (0, turn), group)

    z_upper(0, 0)
    y_all(None, None, 0, 0, 0)
    for side, step in ((0, turn), (1, -turn)):
        for h in range((4, 3)[side]):
            add(("zz", side, h), "z%d" % side, zc[1], 1.7, ("zz", side, h - 1) if h else None, 1,
                (-step * h, 0), (step, 0), h + 1)
            y_all(("zz", side, h), ("zz", side, h), 1, -step * (h + 1), h + 1)
    y_all("zz", None, 1, 0, 0)
    for h in range(4):
        for j in range(4):
            if (j, h) != (0, 0):
                z_upper(j, h)

    left = {}
    for s in streams:
        kind = s.group[0] if s.group[0] == "weight" else s.group[1]
        left[kind] = left.get(kind, 0) + 1
    scaled = []

    def scale_rows():
        each(share, "wait_recv")
        mean = jnp.sum(got_sq[...], axis=0) * (1.0 / (N_SEQ * COLS))
        inverse = lax.rsqrt(mean + EPS)
        eye = iota((128, 128), 0) == iota((128, 128), 1)
        for half in range(2):
            line = jnp.broadcast_to(inverse[half:half + 1], (128, 128))
            column = jnp.sum(jnp.where(eye, line, 0.0), axis=1, keepdims=True)
            scale[pl.ds(128 * half, 128), :] = jnp.broadcast_to(column, (128, 128))

    def multiply(h, n):
        def body(i, carry):
            sign = 1 - 2 * (i // NY)
            d = ((z + sign * h + NZ) % NZ) * NY + i % NY
            gains = gain[0:1, pl.ds(pl.multiple_of(d * COLS, COLS), COLS)]
            wide = jnp.concatenate([scale[...], scale[...]], axis=1)
            normed = (rows[d].astype(F32) * wide * gains).astype(BF16)
            p, half = d // 2, d % 2
            q_at = pl.multiple_of(half * 256, 256)
            kv_at = pl.multiple_of(512 + half * 64, 64)
            acc_q[...] += mm(normed, wbuf[p, pl.ds(q_at, 256), :])
            acc_kv[...] += mm(wbuf[p, pl.ds(kv_at, 64), :], normed, ((1,), (1,)))
            return carry

        lax.fori_loop(0, n, body, 0)

    waiting = [0, 1, 2, 3, 4]

    def row_step(stream, time, later):
        kind = stream.group[0] if stream.group[0] == "weight" else stream.group[1]
        left[kind] -= 1
        if left["weight"]:
            return
        for h in list(waiting):
            if left[h] == 0:
                if not scaled:
                    scaled.append(scale_rows())
                multiply(h, 4 if h in (0, 4) else 8)
                waiting.remove(h)

    plan = schedule(streams, 2.5)
    each(exchange, "start")
    for s in weights:
        if s.parent is None and s.delay == 0.0:
            s.start(started)
    got_main[me] = main[me]
    got_extra[me + 1] = extra[me]
    spot = (blk * 256 + iota((256, HEAD), 0)).astype(F32)
    angle = spot * freq[...]
    cosine[...] = jnp.cos(angle)
    sine[...] = jnp.sin(angle)
    cos_t[...] = cosine[...].T[:64]
    sin_t[...] = sine[...].T[:64]
    sine[...] = jnp.where(iota((256, HEAD), 1) < HEAD // 2, -sine[...], sine[...])
    at = drive(streams, plan, 0, 9.5, started, row_step)
    each(exchange, "wait_recv")

    slots_all = N_SEQ * SLOTS
    slots = got_main[...].reshape(slots_all, COLS)
    heads = (iota((N_SEQ, slots_all), 1) == SLOTS * iota((N_SEQ, slots_all), 0)).astype(BF16)
    metas = mm(heads, slots)
    counts16 = metas[:, :128].astype(BF16)
    source = iota((N_SEQ, slots_all), 0)
    owner = iota((N_SEQ, slots_all), 1) // SLOTS
    before = mm(counts16, (source < owner).astype(BF16), ((0,), (0,)))
    inside = mm(counts16, (source == owner).astype(BF16), ((0,), (0,)))
    rank = (iota((128, slots_all), 1) % SLOTS).astype(F32)
    tails = metas[:, 192:193]
    tails = jnp.concatenate([jnp.zeros((1, 1), F32), tails[:N_SEQ - 1]], axis=0)
    lead_sizes = metas[:, 128:129] + tails
    border = jnp.concatenate(
        [(got_extra[1:N_SEQ + 1, i, :] + got_extra[0:N_SEQ, 2 + i, :]) / lead_sizes
         for i in range(2)], axis=1).astype(BF16)
    spread = (iota((slots_all, N_SEQ), 0) // SLOTS == iota((slots_all, N_SEQ), 1)).astype(BF16)
    first = iota((slots_all, COLS), 0) % SLOTS == 0
    slots = jnp.where(first, mm(spread, border), slots.astype(F32)).astype(BF16)
    ones = jnp.ones((8, COLS), BF16)
    for half in range(2):
        row = (iota((128, slots_all), 0) + 128 * half).astype(F32)
        place = jnp.where(rank < inside, (before + rank == row).astype(F32), 0.0).astype(BF16)
        rows[me, pl.ds(128 * half, 128), :] = mm(place, slots).astype(BF16)
    for half in range(2):
        piece = rows[me, pl.ds(128 * half, 128), :].astype(F32)
        square = piece * piece
        coarse = square.astype(BF16)
        fine = (square - coarse.astype(F32)).astype(BF16)
        across = mm(ones, coarse, ((1,), (1,))) + mm(ones, fine, ((1,), (1,)))
        sq[half:half + 1, :] = across[0:1]

    for s in streams[len(weights):]:
        if s.parent is None:
            s.start(started)
    each(share, "start")
    got_sq[me] = sq[...]
    each(exchange, "wait_send")
    acc_q[...] = jnp.zeros_like(acc_q)
    acc_kv[...] = jnp.zeros_like(acc_kv)
    drive(streams, plan, at, None, started, row_step)
    assert not waiting

    def turn_query(head):
        one = acc_q[:, pl.ds(HEAD * head, HEAD)]
        turned = one * cosine[...] + pltpu.roll(one, HEAD // 2, 1) * sine[...]
        query[head] = turned.astype(BF16)

    kv[...] = acc_kv[...].astype(BF16)
    turn_query(0)
    quad = [
        rdma(kv, parts.at[y], quad_send.at[k], quad_recv.at[k], {"seq": z * NY + (y + k) % NY})
        for k in range(1, NY)
    ]
    for copy in quad:
        copy.start()
    parts[y] = kv[...]
    turn_query(1)
    for copy in quad:
        copy.wait()
    both = jnp.concatenate([parts[i, pl.ds(0, 32), :] for i in range(NY)], axis=0).astype(F32)
    low, high = both[:64], both[64:]
    cos, sin = cos_t[...], sin_t[...]
    keys[blk, pl.ds(0, 64), :] = (low * cos - high * sin).astype(BF16)
    keys[blk, pl.ds(64, 64), :] = (high * cos + low * sin).astype(BF16)
    for i in range(NY):
        keys[blk, pl.ds(128 + 32 * i, 32), :] = parts[i, pl.ds(32, 32), :]

    key_streams = plane_streams(keys, k_send, k_recv, 0.75, [(64 * i, 64) for i in range(4)],
                                "key", 0.0)
    for s in key_streams:
        if s.parent is None:
            s.start(started)

    unit = float(HEAD) ** (-0.5)

    def attend(origin, diagonal):
        for head in range(2):
            s = mm(query[head], keys[origin, pl.ds(0, HEAD), :]) * unit
            if diagonal:
                s = jnp.where(iota((256, 256), 1) <= iota((256, 256), 0), s, -1e30)
            high = jnp.max(s, axis=1, keepdims=True)
            if diagonal:
                new = jnp.broadcast_to(high, (256, HEAD))
            else:
                old = top[head]
                new = jnp.maximum(old, high)
                fade = jnp.exp(old - new)
            w = jnp.exp(s - jnp.concatenate([new, new], axis=1))
            part = w[:, :HEAD] + w[:, HEAD:]
            mix = mm(w.astype(BF16), keys[origin, pl.ds(HEAD, HEAD), :], ((1,), (1,)))
            top[head] = new
            total[head] = part if diagonal else total[head] * fade + part
            acc[head] = mix if diagonal else acc[head] * fade + mix

    attend(blk, True)
    seen, ready = {}, []
    clock = [1.0]

    def attend_earlier(name):
        kind, dx, other = LANDS[name]
        origin = blk_of(yl if kind == 0 else 1 - yl, x + dx, 1 - core if other else core)

        @pl.when(origin < blk)
        def _():
            attend(origin, False)

    def key_step(stream, time, later):
        name = stream.group[1]
        seen[name] = seen.get(name, 0) + 1
        if seen[name] == 4:
            ready.append(name)
        clock[0] = max(clock[0], time)
        while ready and (later is None or clock[0] + 0.6 <= later):
            attend_earlier(ready.pop(0))
            clock[0] += 0.6

    drive(key_streams, schedule(key_streams, 0.0), 0, None, started, key_step)
    for name in ready:
        attend_earlier(name)
    for head in range(2):
        norm = jnp.sum(total[head], axis=1, keepdims=True)
        out[:, pl.ds(HEAD * head, HEAD)] = acc[head] / norm
    for copy in started:
        copy.wait_send()
    each(share, "wait_send")


def on_device(tokens, seg_local, shard_counts, norm_gain, query_weight, keyval_weight):
    vmem = pl.BlockSpec(memory_space=pltpu.VMEM)
    anywhere = pl.BlockSpec(memory_space=pltpu.HBM)
    dma = pltpu.SemaphoreType.DMA
    half = HEAD // 2
    frequency = THETA ** (-((jnp.arange(HEAD, dtype=jnp.int32) % half).astype(F32) * 2.0 / HEAD))
    kv_t = keyval_weight.reshape(512, 64).T
    mixed = pl.pallas_call(
        layer_kernel,
        out_shape=jax.ShapeDtypeStruct((256, 256), F32),
        in_specs=[anywhere] * 7,
        out_specs=vmem,
        scratch_shapes=[
            pltpu.VMEM((1, 128), jnp.int32),
            pltpu.VMEM((1, 128), jnp.int32),
            pltpu.VMEM((1, N_SEQ * COLS), F32),
            pltpu.VMEM((1, HEAD), F32),
            pltpu.VMEM((256, HEAD), F32),
            pltpu.VMEM((256, HEAD), F32),
            pltpu.VMEM((64, 256), F32),
            pltpu.VMEM((64, 256), F32),
            pltpu.VMEM((128, N_SEQ * COLS), BF16),
            pltpu.VMEM((N_SEQ, SLOTS, COLS), BF16),
            pltpu.VMEM((N_SEQ, 4, 128), F32),
            pltpu.VMEM((N_SEQ, SLOTS, COLS), BF16),
            pltpu.VMEM((N_SEQ + 1, 4, 128), F32),
            pltpu.VMEM((2, 128), F32),
            pltpu.VMEM((N_SEQ, 2, 128), F32),
            pltpu.VMEM((N_SEQ, 256, COLS), BF16),
            pltpu.VMEM((N_BLK, 640, 256), BF16),
            pltpu.VMEM((256, 128), F32),
            pltpu.VMEM((256, 256), F32),
            pltpu.VMEM((64, 256), F32),
            pltpu.VMEM((2, 256, HEAD), BF16),
            pltpu.VMEM((64, 256), BF16),
            pltpu.VMEM((NY, 64, 256), BF16),
            pltpu.VMEM((N_BLK, 256, 256), BF16),
            pltpu.VMEM((2, 256, HEAD), F32),
            pltpu.VMEM((2, 256, HEAD), F32),
            pltpu.VMEM((2, 256, HEAD), F32),
            dma((4,)), dma((4,)), dma((3,)),
            dma((2, N_SEQ)), dma((2, N_SEQ)),
            dma((N_SEQ,)), dma((N_SEQ,)),
            dma((62,)), dma((62,)),
            dma((60,)), dma((60,)),
            dma((NY,)), dma((NY,)),
            dma((60,)), dma((60,)),
        ],
        compiler_params=pltpu.CompilerParams(
            collective_id=0, has_side_effects=True, vmem_limit_bytes=63 << 20),
        name="layer",
    )(tokens, seg_local.reshape(1, 128), jnp.broadcast_to(shard_counts, (1, 128)), query_weight,
      kv_t, norm_gain.reshape(1, N_SEQ * COLS), frequency.reshape(1, HEAD))
    return mixed.astype(BF16)


def solution(mesh):
    return jax.shard_map(
        on_device,
        mesh=mesh,
        in_specs=(
            P(("blk", "seq"), None),
            P(("blk", "seq")),
            P("blk", "seq"),
            P(),
            P("blk", "seq"),
            P("blk", None, "seq"),
        ),
        out_specs=P("blk", "seq"),
        check_vma=False,
    )
```

```python
import heapq

import jax
import jax.numpy as jnp
from jax import lax
from jax.experimental import pallas as pl
from jax.experimental.pallas import tpu as pltpu
from jax.sharding import PartitionSpec as P

HEAD = 128
SLOTS = 16
COLS = 256
NZ, NY = 8, 4
NX, NYL, NC = 4, 2, 2
N_SEQ = NZ * NY
N_BLK = NYL * NX * NC
UPPER = 176
THETA = 500000.0
EPS = 1e-05
F32 = jnp.float32
BF16 = jnp.bfloat16
MESH = pl.DeviceIdType.MESH


class Stream:
    def __init__(self, name, link, cost, lag, parent, make, group, delay=0.0):
        self.name, self.link, self.cost, self.lag = name, link, cost, lag
        self.parent, self.make, self.group, self.delay = parent, make, group, delay
        self.begun = False

    def start(self, started):
        self.begun = True
        copy = self.make()
        copy.start()
        started.append(copy)

    def arrive(self):
        self.make().wait_recv()


def schedule(streams, margin):
    by_name = {s.name: i for i, s in enumerate(streams)}
    children = {i: [] for i in range(len(streams))}
    heap, actions = [], []
    for i, s in enumerate(streams):
        if s.parent is None:
            heap.append((s.delay, i))
        else:
            children[by_name[s.parent]].append(i)
    heapq.heapify(heap)
    free = {}
    while heap:
        ready, i = heapq.heappop(heap)
        s = streams[i]
        if s.parent is None and s.delay > 0.0:
            actions.append((ready, 0, i))
        end = max(ready, free.get(s.link, 0.0)) + s.cost
        free[s.link] = end
        actions.append((end + s.lag + (0.0 if children[i] else margin), 1, i))
        for c in children[i]:
            heapq.heappush(heap, (end + s.lag, c))
    return sorted(actions), children


def drive(streams, plan, first, limit, started, after):
    actions, children = plan
    for k in range(first, len(actions)):
        time, kind, i = actions[k]
        if limit is not None and time > limit:
            return k
        if kind == 0:
            if not streams[i].begun:
                streams[i].start(started)
            continue
        streams[i].arrive()
        for c in children[i]:
            streams[c].start(started)
        later = [t for t, kd, j in actions[k + 1:] if kd == 0 or children[j]]
        after(streams[i], time, later[0] if later else None)
    return len(actions)


def rdma(src, dst, send, recv, where):
    return pltpu.make_async_remote_copy(
        src_ref=src, dst_ref=dst, send_sem=send, recv_sem=recv,
        device_id=where, device_id_type=MESH,
    )


def blk_parts():
    blk = lax.axis_index("blk")
    return blk, blk // (NX * NC), (blk // NC) % NX, blk % NC


def blk_of(yl, x, c):
    return (yl * NX + (x + NX) % NX) * NC + c


def plane_peers():
    _, yl, x, c = blk_parts()
    return [blk_of(yl, x + 1, c), blk_of(yl, x - 1, c), blk_of(1 - yl, x, c), blk_of(yl, x, 1 - c)]


PLANE = (
    ("east0", "east", None, 0, 0, 0),
    ("west0", "west", None, 0, 0, 1),
    ("core0", "core", None, 0, 0, 3),
    ("pair", "pair", None, 0, 0, 2),
    ("east1", "east", "east0", 0, -1, 0),
    ("core1", "core", "east0", 0, -1, 3),
    ("core2", "core", "west0", 0, 1, 3),
    ("core3", "core", "east1", 0, 2, 3),
    ("east2", "east", "pair", 1, 0, 0),
    ("west2", "west", "pair", 1, 0, 1),
    ("core4", "core", "pair", 1, 0, 3),
    ("west3", "west", "west2", 1, 1, 1),
    ("core5", "core", "west2", 1, 1, 3),
    ("core6", "core", "east2", 1, -1, 3),
    ("core7", "core", "west3", 1, 2, 3),
)
LANDS = {
    "east0": (0, -1, 0), "west0": (0, 1, 0), "core0": (0, 0, 1), "pair": (1, 0, 0),
    "east1": (0, 2, 0), "core1": (0, -1, 1), "core2": (0, 1, 1), "core3": (0, 2, 1),
    "east2": (1, -1, 0), "west2": (1, 1, 0), "core4": (1, 0, 1), "west3": (1, 2, 0),
    "core5": (1, 1, 1), "core6": (1, -1, 1), "core7": (1, 2, 1),
}


def plane_streams(buf, send, recv, cost, parts, group):
    _, yl, x, c = blk_parts()
    targets = plane_peers()
    streams = []
    for p, (first, size) in enumerate(parts):
        for i, (name, link, parent, kind, dx, target) in enumerate(PLANE):
            origin = blk_of(yl if kind == 0 else 1 - yl, x + dx, c)
            piece = buf.at[origin, pl.ds(first, size)]
            sem = p * len(PLANE) + i

            def make(piece=piece, sem=sem, target=target):
                return rdma(piece, piece, send.at[sem], recv.at[sem], {"blk": targets[target]})

            streams.append(Stream(
                (name, p), link, cost / 5 if link == "core" else cost,
                1.0 if link == "core" else 1.7, None if parent is None else (parent, p), make,
                (group, name)))
    return streams


def mm(a, b, dims=((1,), (0,))):
    return lax.dot_general(a, b, (dims, ((), ())), preferred_element_type=F32)


def iota(shape, axis):
    return lax.broadcasted_iota(jnp.int32, shape, axis)


def layer_kernel(
    tokens, seg_hbm, count_hbm, q_weight, kv_weight, gain_hbm, freq_hbm, out,
    seg, count, gain, freq, cosine, sine, cos_t, sin_t, tok, main, extra, got_main, got_extra, sq, got_sq, rows, wbuf, scale, acc_q, acc_kv,
    query, kv, parts, keys, top, total, acc,
    small_sem, tok_sem, own_sem, a2a_send, a2a_recv, sq_send, sq_recv, r_send, r_recv,
    w_send, w_recv, quad_send, quad_recv, k_send, k_recv,
):
    me = lax.axis_index("seq")
    z, y = me // NY, me % NY
    blk, yl, x, core = blk_parts()
    turn = 1 - 2 * core

    def seq_of(zz, yy):
        return ((zz + 2 * NZ) % NZ) * NY + (yy + 2 * NY) % NY

    barrier = pltpu.get_barrier_semaphore()

    def greet(k, carry):
        far = (k + 13) % (N_SEQ - 1) + 1
        pl.semaphore_signal(barrier, inc=1, device_id={"seq": (me + far) % N_SEQ},
                            device_id_type=MESH)
        return carry

    chunk = N_SEQ * COLS // 4
    token_loads = [
        pltpu.make_async_copy(tokens.at[:, pl.ds(i * chunk, chunk)],
                              tok.at[:, pl.ds(i * chunk, chunk)], tok_sem.at[i])
        for i in range(4)
    ]
    own_loads = [
        pltpu.make_async_copy(q_weight, wbuf.at[blk, pl.ds(0, 512)], own_sem.at[0]),
        pltpu.make_async_copy(kv_weight.at[:, pl.ds(0, 256)], wbuf.at[blk, pl.ds(512, 64)],
                              own_sem.at[1]),
        pltpu.make_async_copy(kv_weight.at[:, pl.ds(256, 256)], wbuf.at[blk, pl.ds(576, 64)],
                              own_sem.at[2]),
    ]
    smalls = [
        pltpu.make_async_copy(src, dst, small_sem.at[i])
        for i, (src, dst) in enumerate((
            (seg_hbm, seg), (count_hbm, count), (gain_hbm, gain), (freq_hbm, freq)))
    ]
    for load in smalls[:2] + token_loads + own_loads + smalls[2:]:
        load.start()
    lax.fori_loop(1, N_SEQ, greet, 0)
    for peer in plane_peers():
        pl.semaphore_signal(barrier, inc=1, device_id={"blk": peer}, device_id_type=MESH)

    for load in smalls[:2]:
        load.wait()
    slot = iota((SLOTS, 128), 0)
    member = (seg[...] == slot).astype(F32)
    sizes = jnp.sum(member, axis=1, keepdims=True)
    member = member.astype(BF16)
    is_tail = (slot == count[...]).astype(F32)
    tail_pick = is_tail[:, 0:1]
    tail_size = jnp.sum(sizes * is_tail, axis=0, keepdims=True)
    safe = jnp.maximum(sizes, 1.0)
    meta = jnp.concatenate(
        [count[...].astype(F32), jnp.broadcast_to(sizes[0:1], (1, 64)), tail_size[:, :64]], axis=1)
    top_row = iota((SLOTS, COLS), 0) == 0

    for i in range(4):
        token_loads[i].wait()
        for d in range(8 * i, 8 * i + 8):
            sums = mm(member, tok[:, pl.ds(d * COLS, COLS)])
            main[d] = jnp.where(top_row, meta, sums / safe).astype(BF16)
            tail = jnp.sum(sums * tail_pick, axis=0, keepdims=True)
            extra[d] = jnp.concatenate(
                [sums[0:1, :128], sums[0:1, 128:], tail[:, :128], tail[:, 128:]], axis=0)
    got_extra[0] = jnp.zeros((4, 128), F32)
    for load in own_loads + smalls[2:]:
        load.wait()
    pl.semaphore_wait(barrier, N_SEQ - 1 + 4)

    def exchange(k):
        to = (me + k) % N_SEQ
        return (
            rdma(main.at[to], got_main.at[me], a2a_send.at[0, k], a2a_recv.at[0, k], {"seq": to}),
            rdma(extra.at[to], got_extra.at[me + 1], a2a_send.at[1, k], a2a_recv.at[1, k],
                 {"seq": to}),
        )

    def share(k):
        return (rdma(sq, got_sq.at[me], sq_send.at[k], sq_recv.at[k], {"seq": (me + k) % N_SEQ}),)

    def each(copies, what):
        def body(k, carry):
            for copy in copies((k + 13) % (N_SEQ - 1) + 1):
                getattr(copy, what)()
            return carry

        lax.fori_loop(1, N_SEQ, body, 0)

    started = []
    weights = plane_streams(wbuf, w_send, w_recv, 1.9, [(160 * i, 160) for i in range(4)],
                            "weight")
    streams = list(weights)
    counter = [0]

    def add(name, link, cost, lag, parent, part, origin, target, group):
        sem = counter[0]
        counter[0] += 1
        at, size = ((0, UPPER), (UPPER, 256 - UPPER))[part]
        piece = rows.at[seq_of(z + origin[0], y + origin[1]), pl.ds(at, size)]
        where = {"seq": seq_of(z + target[0], y + target[1])}

        def make():
            return rdma(piece, piece, r_send.at[sem], r_recv.at[sem], where)

        streams.append(Stream(name, link, cost, lag, parent, make, ("row", group),
                              13.0 if parent is None else 0.0))

    zc = (0.01138 * UPPER, 0.01138 * (256 - UPPER))
    yc = (0.0125 * UPPER, 0.0125 * (256 - UPPER))
    dys = (0, -turn, turn, 2)
    hops = ((4, 3), (3, 4), (4, 3), (3, 4))
    own = ("yA", "yB", "yC")

    def z_upper(j, h):
        for side, step in ((0, 1), (1, -1)):
            if h < hops[j][side]:
                parent = ("z", j, side, h - 1) if h else (None if j == 0 else own[j - 1])
                add(("z", j, side, h), "z%d" % side, zc[0], 1.7, parent, 0,
                    (-step * h, dys[j]), (step, 0), h + 1)

    def y_all(tag, parent, part, dz, group):
        names = own if tag is None else tuple((n, tag) for n in own)
        add(names[0], "y", yc[part], 2.4, parent, part, (dz, 0), (0, turn), group)
        add(names[1], "y", yc[part], 2.4, parent, part, (dz, 0), (0, -turn), group)
        add(names[2], "y", yc[part], 2.4, names[0], part, (dz, -turn), (0, turn), group)

    z_upper(0, 0)
    y_all(None, None, 0, 0, 0)
    for side, step in ((0, turn), (1, -turn)):
        for h in range((4, 3)[side]):
            add(("zz", side, h), "z%d" % side, zc[1], 1.7, ("zz", side, h - 1) if h else None, 1,
                (-step * h, 0), (step, 0), h + 1)
            y_all(("zz", side, h), ("zz", side, h), 1, -step * (h + 1), h + 1)
    y_all("zz", None, 1, 0, 0)
    for h in range(4):
        for j in range(4):
            if (j, h) != (0, 0):
                z_upper(j, h)

    left = {}
    for s in streams:
        kind = s.group[0] if s.group[0] == "weight" else s.group[1]
        left[kind] = left.get(kind, 0) + 1
    scaled = []

    def scale_rows():
        each(exchange, "wait_send")
        each(share, "wait_recv")
        each(share, "wait_send")
        mean = jnp.sum(got_sq[...], axis=0) * (1.0 / (N_SEQ * COLS))
        inverse = lax.rsqrt(mean + EPS)
        eye = iota((128, 128), 0) == iota((128, 128), 1)
        for half in range(2):
            line = jnp.broadcast_to(inverse[half:half + 1], (128, 128))
            column = jnp.sum(jnp.where(eye, line, 0.0), axis=1, keepdims=True)
            scale[pl.ds(128 * half, 128), :] = jnp.broadcast_to(column, (128, 128))

    def multiply(h, n):
        def body(i, carry):
            sign = 1 - 2 * (i // NY)
            d = ((z + sign * h + NZ) % NZ) * NY + i % NY
            gains = gain[0:1, pl.ds(pl.multiple_of(d * COLS, COLS), COLS)]
            wide = jnp.concatenate([scale[...], scale[...]], axis=1)
            normed = (rows[d].astype(F32) * wide * gains).astype(BF16)
            p, half = d // 2, d % 2
            q_at = pl.multiple_of(half * 256, 256)
            kv_at = pl.multiple_of(512 + half * 64, 64)
            acc_q[...] += mm(normed, wbuf[p, pl.ds(q_at, 256), :])
            acc_kv[...] += mm(wbuf[p, pl.ds(kv_at, 64), :], normed, ((1,), (1,)))
            return carry

        lax.fori_loop(0, n, body, 0)

    waiting = [0, 1, 2, 3, 4]

    def row_step(stream, time, later):
        kind = stream.group[0] if stream.group[0] == "weight" else stream.group[1]
        left[kind] -= 1
        if left["weight"]:
            return
        for h in list(waiting):
            if left[h] == 0:
                if not scaled:
                    scaled.append(scale_rows())
                multiply(h, 4 if h in (0, 4) else 8)
                waiting.remove(h)

    plan = schedule(streams, 2.5)
    each(exchange, "start")
    for s in weights:
        if s.parent is None and s.delay == 0.0:
            s.start(started)
    got_main[me] = main[me]
    got_extra[me + 1] = extra[me]
    spot = (blk * 256 + iota((256, HEAD), 0)).astype(F32)
    angle = spot * freq[...]
    cosine[...] = jnp.cos(angle)
    sine[...] = jnp.sin(angle)
    cos_t[...] = cosine[...].T[:64]
    sin_t[...] = sine[...].T[:64]
    sine[...] = jnp.where(iota((256, HEAD), 1) < HEAD // 2, -sine[...], sine[...])
    at = drive(streams, plan, 0, 9.5, started, row_step)
    each(exchange, "wait_recv")

    slots_all = N_SEQ * SLOTS
    slots = got_main[...].reshape(slots_all, COLS)
    heads = (iota((N_SEQ, slots_all), 1) == SLOTS * iota((N_SEQ, slots_all), 0)).astype(BF16)
    metas = mm(heads, slots)
    counts16 = metas[:, :128].astype(BF16)
    source = iota((N_SEQ, slots_all), 0)
    owner = iota((N_SEQ, slots_all), 1) // SLOTS
    before = mm(counts16, (source < owner).astype(BF16), ((0,), (0,)))
    inside = mm(counts16, (source == owner).astype(BF16), ((0,), (0,)))
    rank = (iota((128, slots_all), 1) % SLOTS).astype(F32)
    tails = metas[:, 192:193]
    tails = jnp.concatenate([jnp.zeros((1, 1), F32), tails[:N_SEQ - 1]], axis=0)
    lead_sizes = metas[:, 128:129] + tails
    border = jnp.concatenate(
        [(got_extra[1:N_SEQ + 1, i, :] + got_extra[0:N_SEQ, 2 + i, :]) / lead_sizes
         for i in range(2)], axis=1).astype(BF16)
    spread = (iota((slots_all, N_SEQ), 0) // SLOTS == iota((slots_all, N_SEQ), 1)).astype(BF16)
    first = iota((slots_all, COLS), 0) % SLOTS == 0
    slots = jnp.where(first, mm(spread, border), slots.astype(F32)).astype(BF16)
    ones = jnp.ones((8, COLS), BF16)
    for half in range(2):
        row = (iota((128, slots_all), 0) + 128 * half).astype(F32)
        place = jnp.where(rank < inside, (before + rank == row).astype(F32), 0.0).astype(BF16)
        rows[me, pl.ds(128 * half, 128), :] = mm(place, slots).astype(BF16)
    for half in range(2):
        piece = rows[me, pl.ds(128 * half, 128), :].astype(F32)
        square = piece * piece
        coarse = square.astype(BF16)
        fine = (square - coarse.astype(F32)).astype(BF16)
        across = mm(ones, coarse, ((1,), (1,))) + mm(ones, fine, ((1,), (1,)))
        sq[half:half + 1, :] = across[0:1]

    for s in streams[len(weights):]:
        if s.parent is None:
            s.start(started)
    each(share, "start")
    got_sq[me] = sq[...]
    acc_q[...] = jnp.zeros_like(acc_q)
    acc_kv[...] = jnp.zeros_like(acc_kv)
    drive(streams, plan, at, None, started, row_step)
    assert not waiting

    def turn_query(head):
        one = acc_q[:, pl.ds(HEAD * head, HEAD)]
        turned = one * cosine[...] + pltpu.roll(one, HEAD // 2, 1) * sine[...]
        query[head] = turned.astype(BF16)

    kv[...] = acc_kv[...].astype(BF16)
    turn_query(0)
    quad = [
        rdma(kv, parts.at[y], quad_send.at[k], quad_recv.at[k], {"seq": z * NY + (y + k) % NY})
        for k in (2, 1, 3)
    ]
    for copy in quad:
        copy.start()
    parts[y] = kv[...]
    turn_query(1)
    for copy in quad:
        copy.wait()
    both = jnp.concatenate([parts[i, pl.ds(0, 32), :] for i in range(NY)], axis=0).astype(F32)
    low, high = both[:64], both[64:]
    cos, sin = cos_t[...], sin_t[...]
    keys[blk, pl.ds(0, 64), :] = (low * cos - high * sin).astype(BF16)
    keys[blk, pl.ds(64, 64), :] = (high * cos + low * sin).astype(BF16)
    for i in range(NY):
        keys[blk, pl.ds(128 + 32 * i, 32), :] = parts[i, pl.ds(32, 32), :]

    key_streams = plane_streams(keys, k_send, k_recv, 0.75, [(64 * i, 64) for i in range(4)],
                                "key")
    key_started = []
    for s in key_streams:
        if s.parent is None:
            s.start(key_started)

    unit = float(HEAD) ** (-0.5)

    def attend(origin, diagonal):
        for head in range(2):
            s = mm(query[head], keys[origin, pl.ds(0, HEAD), :]) * unit
            if diagonal:
                s = jnp.where(iota((256, 256), 1) <= iota((256, 256), 0), s, -1e30)
            high = jnp.max(s, axis=1, keepdims=True)
            if diagonal:
                new = jnp.broadcast_to(high, (256, HEAD))
            else:
                old = top[head]
                new = jnp.maximum(old, high)
                fade = jnp.exp(old - new)
            w = jnp.exp(s - jnp.concatenate([new, new], axis=1))
            part = w[:, :HEAD] + w[:, HEAD:]
            mix = mm(w.astype(BF16), keys[origin, pl.ds(HEAD, HEAD), :], ((1,), (1,)))
            top[head] = new
            total[head] = part if diagonal else total[head] * fade + part
            acc[head] = mix if diagonal else acc[head] * fade + mix

    attend(blk, True)
    for copy in started:
        copy.wait_send()
    seen, ready = {}, []
    clock = [1.0]

    def attend_earlier(name):
        kind, dx, other = LANDS[name]
        origin = blk_of(yl if kind == 0 else 1 - yl, x + dx, 1 - core if other else core)

        @pl.when(origin < blk)
        def _():
            attend(origin, False)

    def key_step(stream, time, later):
        name = stream.group[1]
        seen[name] = seen.get(name, 0) + 1
        if seen[name] == 4:
            ready.append(name)
        clock[0] = max(clock[0], time)
        while ready and (later is None or clock[0] + 0.6 <= later):
            attend_earlier(ready.pop(0))
            clock[0] += 0.6

    drive(key_streams, schedule(key_streams, 0.0), 0, None, key_started, key_step)
    for name in ready:
        attend_earlier(name)
    for head in range(2):
        norm = jnp.sum(total[head], axis=1, keepdims=True)
        out[:, pl.ds(HEAD * head, HEAD)] = acc[head] / norm
    for copy in key_started:
        copy.wait_send()


def on_device(tokens, seg_local, shard_counts, norm_gain, query_weight, keyval_weight):
    vmem = pl.BlockSpec(memory_space=pltpu.VMEM)
    anywhere = pl.BlockSpec(memory_space=pltpu.HBM)
    dma = pltpu.SemaphoreType.DMA
    half = HEAD // 2
    frequency = THETA ** (-((jnp.arange(HEAD, dtype=jnp.int32) % half).astype(F32) * 2.0 / HEAD))
    kv_t = keyval_weight.reshape(512, 64).T
    mixed = pl.pallas_call(
        layer_kernel,
        out_shape=jax.ShapeDtypeStruct((256, 256), F32),
        in_specs=[anywhere] * 7,
        out_specs=vmem,
        scratch_shapes=[
            pltpu.VMEM((1, 128), jnp.int32),
            pltpu.VMEM((1, 128), jnp.int32),
            pltpu.VMEM((1, N_SEQ * COLS), F32),
            pltpu.VMEM((1, HEAD), F32),
            pltpu.VMEM((256, HEAD), F32),
            pltpu.VMEM((256, HEAD), F32),
            pltpu.VMEM((64, 256), F32),
            pltpu.VMEM((64, 256), F32),
            pltpu.VMEM((128, N_SEQ * COLS), BF16),
            pltpu.VMEM((N_SEQ, SLOTS, COLS), BF16),
            pltpu.VMEM((N_SEQ, 4, 128), F32),
            pltpu.VMEM((N_SEQ, SLOTS, COLS), BF16),
            pltpu.VMEM((N_SEQ + 1, 4, 128), F32),
            pltpu.VMEM((2, 128), F32),
            pltpu.VMEM((N_SEQ, 2, 128), F32),
            pltpu.VMEM((N_SEQ, 256, COLS), BF16),
            pltpu.VMEM((N_BLK, 640, 256), BF16),
            pltpu.VMEM((256, 128), F32),
            pltpu.VMEM((256, 256), F32),
            pltpu.VMEM((64, 256), F32),
            pltpu.VMEM((2, 256, HEAD), BF16),
            pltpu.VMEM((64, 256), BF16),
            pltpu.VMEM((NY, 64, 256), BF16),
            pltpu.VMEM((N_BLK, 256, 256), BF16),
            pltpu.VMEM((2, 256, HEAD), F32),
            pltpu.VMEM((2, 256, HEAD), F32),
            pltpu.VMEM((2, 256, HEAD), F32),
            dma((4,)), dma((4,)), dma((3,)),
            dma((2, N_SEQ)), dma((2, N_SEQ)),
            dma((N_SEQ,)), dma((N_SEQ,)),
            dma((62,)), dma((62,)),
            dma((60,)), dma((60,)),
            dma((NY,)), dma((NY,)),
            dma((60,)), dma((60,)),
        ],
        compiler_params=pltpu.CompilerParams(
            collective_id=0, has_side_effects=True, vmem_limit_bytes=63 << 20),
        name="layer",
    )(tokens, seg_local.reshape(1, 128), jnp.broadcast_to(shard_counts, (1, 128)), query_weight,
      kv_t, norm_gain.reshape(1, N_SEQ * COLS), frequency.reshape(1, HEAD))
    return mixed.astype(BF16)


def solution(mesh):
    return jax.shard_map(
        on_device,
        mesh=mesh,
        in_specs=(
            P(("blk", "seq"), None),
            P(("blk", "seq")),
            P("blk", "seq"),
            P(),
            P("blk", "seq"),
            P("blk", None, "seq"),
        ),
        out_specs=P("blk", "seq"),
        check_vma=False,
    )
```
